32 devices in a mesh: aux: 8 (over z, y), orb: 4 (over x, core).
Axes of the slice: x: 2, y: 2, z: 4, core: 2. Of those that a mesh axis runs over, the one named last changes fastest.
Arguments:
- integrals: bfloat16 [16384, 10240], P('aux', 'orb'), may hold values from -0.29882812 to 0.29882812
- factors: bfloat16 [6, 128, 16384], P(None, 'orb', 'aux'), may hold values from -0.59765625 to 0.59765625
- gap_ov: float32 [10240], P('orb'), may hold values from 0.5 to 8
- gap_block: float32 [6, 128], P(None, 'orb'), may hold values from 0.5 to 8
Outputs:
- density: float32 [16384, 10240], P('aux', 'orb')
The draws below stay inside these ranges and needn't reach their ends.
All inputs are finite; a program needn't handle non-finite values.
Results may differ from the reference program's by a relative error of at most 0.006.
Values may be sent and summed in bfloat16 or wider, within the bound.
No kernel may reach another device: no remote copies, remote signals or barrier semaphores. Data moves between devices by JAX's collectives and lax.ppermute only.
A program may use at most 128 MiB of HBM per device.

```python
import math
import jax
import jax.numpy as jnp
from jax import lax

BLOCK = 128
NBLOCK = 6
NAUX = 16384
NOV = 10240


def level_of(rng, extent, cuts, smallest, top_value):
    factor_of, own = 1.0, jax.random.fold_in(rng, 6)
    for dim, blocks in cuts:
        draws = jnp.exp(jax.random.uniform(jax.random.fold_in(own, dim), (blocks,), jnp.float32, smallest / len(cuts), top_value / len(cuts)))
        factor_of = factor_of * jnp.repeat(draws, extent[dim] // blocks).reshape([-1 if axis == dim else 1 for axis in range(len(extent))])
    return factor_of


def centred(rng, shape, width, limit, pieces=(), kind=jnp.bfloat16):
    array = width * jax.random.normal(rng, shape, jnp.float32)
    if pieces:
        array = array * level_of(rng, shape, pieces, -0.22, 0.18)
    return jnp.clip(array, -limit, limit).astype(kind)


def setup_inputs(seed: int = 0) -> dict:
    seeds = jax.random.split(jax.random.key(seed), 5)
    integrals = centred(seeds[0], (NAUX, NOV), 0.05, 0.29882812, ((0, 8), (1, 4)))
    factors = centred(seeds[1], (NBLOCK, BLOCK, NAUX), 0.1, 0.59765625, ((1, 4), (2, 8)))
    gap_ov = jnp.clip(jnp.exp(math.log(8.0) - 2.7725887 * jax.random.uniform(seeds[2], (NOV,), jnp.float32) ** level_of(seeds[2], (NOV,), ((0, 4),), -0.2, 0.2)), 0.5, 8.0)
    gap_block = jnp.clip(jnp.exp(math.log(8.0) - 2.7725887 * jax.random.uniform(seeds[3], (NBLOCK, BLOCK), jnp.float32) ** level_of(seeds[3], (NBLOCK, BLOCK), ((1, 4),), -0.2, 0.2)), 0.5, 8.0)
    return {"integrals": integrals, "factors": factors, "gap_ov": gap_ov, "gap_block": gap_block}


def reference(integrals, factors, gap_ov, gap_block):
    amps = []
    for index in range(NBLOCK):
        pair = lax.dot_general(integrals, factors[index], (((0,), (1,)), ((), ())), preferred_element_type=jnp.float32)
        denom = gap_ov[:, None] + gap_block[index][None, :]
        amps.append((pair / denom).astype(jnp.bfloat16))
    amp_all = jnp.concatenate(amps, axis=1)
    factor = factors.reshape(NBLOCK * BLOCK, NAUX)
    density = lax.dot_general(factor, amp_all, (((0,), (1,)), ((), ())), preferred_element_type=jnp.float32)
    return density
```

```python
import functools

import jax
import jax.numpy as jnp
from jax import lax
from jax.experimental import pallas as pl
from jax.experimental.pallas import tpu as pltpu
from jax.sharding import PartitionSpec as P


LANES = 128
GRANT = 20 << 20
f32, bf16 = jnp.float32, jnp.bfloat16
ANYWHERE = pl.BlockSpec(memory_space=pl.ANY)
NEAR = pl.BlockSpec(memory_space=pltpu.VMEM)
FAR = pl.BlockSpec(memory_space=pltpu.HBM)
SCALARS = pl.BlockSpec(memory_space=pltpu.SMEM)


def swap(value, axis, size, bit):
    return lax.ppermute(value, axis, [(i, i ^ bit) for i in range(size)])


def bit_of(index, bit):
    return ((index // bit) % 2).astype(jnp.int32)


class Chain:
    def __init__(self, bits):
        self.bits = bits
        self.last = None

    def __call__(self, body, operands, out_shape, in_specs=None, out_specs=None, grid=(), scratch=(), aliases=None, flops=0, moved=0, grant=GRANT):
        count = len(operands)
        tail = [] if self.last is None or any(self.last is x for x in operands) else [self.last]
        in_specs = in_specs or [NEAR] * count

        def wrapped(bits_ref, *refs):
            body(bits_ref, *refs[:count], *refs[count + len(tail) :])

        spec = dict(
            grid=grid,
            in_specs=[*([] if grid else [SCALARS]), *in_specs, *[ANYWHERE for _ in tail]],
            out_specs=out_specs or jax.tree.map(lambda _: NEAR, out_shape),
            scratch_shapes=list(scratch),
        )
        if grid:
            spec = dict(grid_spec=pltpu.PrefetchScalarGridSpec(num_scalar_prefetch=1, **spec))
        out = pl.pallas_call(
            wrapped,
            out_shape=out_shape,
            **spec,
            input_output_aliases={i + 1: o for i, o in (aliases or {}).items()},
            compiler_params=pltpu.CompilerParams(
                dimension_semantics=("arbitrary",) * len(grid) or None, vmem_limit_bytes=grant
            ),
            cost_estimate=pl.CostEstimate(flops=flops, bytes_accessed=moved, transcendentals=0),
        )(self.bits, *operands, *tail)
        self.last = out[0] if isinstance(out, (tuple, list)) else out
        return out


def rows_at(block, size):
    return pl.ds(pl.multiple_of(block * size, size), size)


def load_body(chunks, bits, in_ref, out_ref, sems):
    size = in_ref.shape[0] // chunks
    spans = [pl.ds(k * size, size) for k in range(chunks)]
    copies = [pltpu.make_async_copy(in_ref.at[s], out_ref.at[s], sems.at[k]) for k, s in enumerate(spans)]
    for copy in copies:
        copy.start()
    for copy in copies:
        copy.wait()


def load(chain, value):
    chunks = 8 if value.shape[0] % 128 == 0 else 1
    return chain(
        functools.partial(load_body, chunks), [value], jax.ShapeDtypeStruct(value.shape, value.dtype), in_specs=[FAR],
        scratch=[pltpu.SemaphoreType.DMA((chunks,))], moved=2 * value.size,
    )


def multiply_body(count, first, slot, flip, slot_rows, chunks, width, bits, *refs):
    pieces, b_ref, rest = refs[:count], refs[count], refs[count + 1 :]
    acc, outs = rest[-1], rest[:-1]
    depth = b_ref.shape[0]
    chunk = depth // chunks
    if first is None:
        columns = slice(None)
    else:
        side = 1 - bits[slot] if flip else bits[slot]
        columns = pl.ds(pl.multiple_of(first + side * width, LANES), width)
    for k in range(chunks):
        span = slice(k * chunk, (k + 1) * chunk)
        rows = jnp.concatenate([ref[:, span] for ref in pieces], axis=0)
        term = jnp.dot(rows, b_ref[span, columns], preferred_element_type=f32)
        if k:
            acc[...] += term
        else:
            acc[...] = term
    if len(outs) == 1:
        outs[0][...] = acc[...].astype(bf16)
    else:
        in_ref, send_ref, keep_ref = outs
        half = keep_ref.shape[0]
        mine = bits[slot_rows]
        other, own = rows_at(1 - mine, half), rows_at(mine, half)
        send_ref[...] = (acc[other, :] + in_ref[other, :].astype(f32)).astype(bf16)
        keep_ref[...] = acc[own, :] + in_ref[own, :].astype(f32)


def multiply(chain, integrals, pieces, first, slot, flip, slot_rows, width, arrived=None):
    depth = integrals.shape[0]
    chunks = 2 if depth % (2 * LANES) == 0 else 1
    rows = pieces[0].shape[0] * len(pieces)
    if width % LANES:
        side = 1 - chain.bits[slot] if flip else chain.bits[slot]
        integrals = lax.dynamic_slice_in_dim(integrals, first + side * width, width, axis=1)
        first = None
    extra = [] if arrived is None else [arrived]
    half = rows // 2
    return chain(
        functools.partial(multiply_body, len(pieces), first, slot, flip, slot_rows, chunks, width),
        [*pieces, integrals, *extra],
        jax.ShapeDtypeStruct((rows, width), bf16) if arrived is None
        else (jax.ShapeDtypeStruct((half, width), bf16), jax.ShapeDtypeStruct((half, width), f32)),
        scratch=[pltpu.VMEM((rows, width), f32)],
        flops=2 * rows * width * depth, moved=2 * depth * (rows + width) + 4 * rows * width,
    )


def add_half_body(slot, bits, keep_ref, in_ref, send_ref, out_ref):
    half = out_ref.shape[0]
    mine = bits[slot]
    other, own = rows_at(1 - mine, half), rows_at(mine, half)
    send_ref[...] = (keep_ref[other, :] + in_ref[other, :].astype(f32)).astype(bf16)
    out_ref[...] = keep_ref[own, :] + in_ref[own, :].astype(f32)


def add_body(bits, keep_ref, in_ref, send_ref, out_ref):
    total = keep_ref[...] + in_ref[...].astype(f32)
    send_ref[...] = total.astype(bf16)
    out_ref[...] = total


def add(chain, keep, got, slot=None):
    rows, width = keep.shape
    out = rows if slot is None else rows // 2
    return chain(
        add_body if slot is None else functools.partial(add_half_body, slot), [keep, got],
        (jax.ShapeDtypeStruct((out, width), bf16), jax.ShapeDtypeStruct((out, width), f32)),
        moved=12 * rows * width,
    )


def divide_body(first, slot, slots, bits, keep_ref, in_ref, ov_ref, gb_ref, out_ref):
    rows, width = keep_ref.shape
    total = keep_ref[...] + in_ref[...].astype(f32)
    block = 0
    for s in slots:
        block = block * 2 + bits[s]
    gb = gb_ref[rows_at(block, rows), :][:, :1]
    ov = ov_ref[...] if first is None else ov_ref[:, pl.ds(pl.multiple_of(first + bits[slot] * width, LANES), width)]
    out_ref[...] = (total / (gb + ov)).astype(bf16)


def divide(chain, keep, got, ov, gaps, first, slot, slots):
    rows, width = keep.shape
    if width % LANES:
        ov = lax.dynamic_slice_in_dim(ov, first + chain.bits[slot] * width, width, axis=1)
        first = None
    return chain(
        functools.partial(divide_body, first, slot, slots), [keep, got, ov, gaps],
        jax.ShapeDtypeStruct((rows, width), bf16), moved=8 * rows * width,
    )


def join_body(slot, bits, own_ref, in_ref, out_ref):
    rows = own_ref.shape[0]
    out_ref[rows_at(bits[slot], rows), :] = own_ref[...]
    out_ref[rows_at(1 - bits[slot], rows), :] = in_ref[...]


def join(chain, own, got, slot):
    rows, width = own.shape
    return chain(
        functools.partial(join_body, slot), [own, got],
        jax.ShapeDtypeStruct((2 * rows, width), bf16), moved=8 * rows * width,
    )


def stack_body(count, bits, *refs):
    rows = refs[0].shape[0]
    for i in range(count):
        refs[count][i * rows : (i + 1) * rows, :] = refs[i][...]


def unpack_body(count, depth, bits, *refs):
    rows = refs[0].shape[0]
    for i in range(count):
        high, low = refs[i][:, depth : depth + LANES], refs[i][:, depth + LANES :]
        refs[count][i * rows : (i + 1) * rows, :] = high.astype(f32) + low.astype(f32)


def stack(chain, parts, depth=None):
    rows = parts[0].shape[0]
    body = functools.partial(stack_body, len(parts)) if depth is None else functools.partial(unpack_body, len(parts), depth)
    return chain(body, parts, jax.ShapeDtypeStruct((rows * len(parts), LANES), f32))


def hold_body(bits, in_ref, out_ref):
    pass


def hold(chain, value):
    return chain(
        hold_body, [value], jax.ShapeDtypeStruct(value.shape, value.dtype), in_specs=[ANYWHERE], out_specs=ANYWHERE,
        aliases={0: 0},
    )


def density_body(count, groups, parts, tile, bits, *refs):
    pieces, amps, out_ref = refs[:count], refs[count : count + groups * len(parts)], refs[-1]
    start = pl.multiple_of(pl.program_id(0) * tile, tile)
    factor = jnp.concatenate([ref[:, pl.ds(start, tile)] for ref in pieces], axis=0)
    for i, part in enumerate(parts):
        amp = jnp.concatenate([ref[...] for ref in amps[i * groups : (i + 1) * groups]], axis=0)
        result = lax.dot_general(factor, amp, (((0,), (0,)), ((), ())), preferred_element_type=f32)
        if len(parts) == 1:
            out_ref[...] = result
        else:
            slot, flip = part
            side = 1 - bits[slot] if flip else bits[slot]
            width = result.shape[1]
            out_ref[:, pl.ds(pl.multiple_of(side * width, LANES), width)] = result


def finish(chain, pieces, amps, parts, first, cols, depth, previous):
    groups = len(amps) // len(parts)
    rows, width = amps[0].shape
    total, span = rows * groups, width * len(parts)
    tile = 512 if depth % 512 == 0 else depth
    operands = [*pieces, *amps]
    in_specs = [NEAR] * len(operands)
    aliases = {}
    if previous is not None:
        aliases = {len(operands): 0}
        in_specs.append(ANYWHERE)
        operands.append(previous)

    def place(i, bits):
        if len(parts) > 1 or parts[0] is None:
            return i, first // span
        slot, flip = parts[0]
        return i, first // span + (1 - bits[slot] if flip else bits[slot])

    return chain(
        functools.partial(density_body, len(pieces), groups, parts, tile), operands,
        jax.ShapeDtypeStruct((depth, cols), f32), in_specs=in_specs,
        out_specs=pl.BlockSpec((tile, span), place), grid=(depth // tile,), aliases=aliases,
        flops=2 * total * span * depth, moved=2 * total * (span + depth) + 4 * depth * span,
    )


class Unit:
    def __init__(self, chain, env, half, first, width, order):
        self.chain, self.env, self.half, self.first, self.width, self.order = chain, env, half, first, width, order

    def swap(self, value, s):
        return swap(value, "aux", self.env["aux"], 1 << self.order[s])

    def multiply(self, flip, got=None):
        return multiply(
            self.chain, self.env["integrals"], self.env["halves"][self.half], self.first, self.order[0], flip,
            self.order[1], self.width, got,
        )

    def start(self):
        self.got = self.swap(self.multiply(True), 0)

    def keep(self):
        send, self.kept = self.multiply(False, self.got)
        self.got = self.swap(send, 1)

    def add(self):
        last = len(self.order) - 1
        for s in range(2, last):
            send, self.kept = add(self.chain, self.kept, self.got, self.order[s])
            self.got = self.swap(send, s)
        send, self.kept = add(self.chain, self.kept, self.got)
        self.got = self.swap(send, last)

    def divide(self):
        env, order = self.env, self.order
        self.amp = divide(
            self.chain, self.kept, self.got, env["ov"], env["gaps"][self.half], self.first, order[0], order[1:-1]
        )
        for s in range(len(order) - 2, 1, -1):
            self.amp = join(self.chain, self.amp, self.swap(self.amp, s), order[s])
        self.got = self.swap(self.amp, 1)

    def join(self):
        self.amp = join(self.chain, self.amp, self.got, self.order[1])
        self.other = self.swap(self.amp, 0)


def local(aux, orb, integrals, factors, gap_ov, gap_block):
    depth, cols = integrals.shape
    rows_each = factors.shape[0] * factors.shape[1]
    me = lax.axis_index("aux").astype(jnp.int32)
    steps = (aux - 1).bit_length()
    bits = (me >> jnp.arange(steps, dtype=jnp.int32)) & 1
    chain = Chain(bits)

    own = factors.reshape(rows_each, depth)
    gap = jnp.broadcast_to(gap_block.reshape(rows_each, 1), (rows_each, LANES))

    def expand(first):
        pieces, bit = [first], 1
        while bit < orb // 2:
            pieces += [swap(piece, "orb", orb, bit) for piece in pieces]
            bit *= 2
        return pieces

    order = tuple(range(steps))
    env = dict(aux=aux, integrals=load(chain, integrals), ov=gap_ov.reshape(1, cols), halves=[expand(own), None], gaps=[None, None])
    high = gap.astype(bf16)
    low = (gap - high.astype(f32)).astype(bf16)
    far_own = swap(jnp.concatenate([own, high, low], axis=1), "orb", orb, orb // 2)
    gap_parts = expand(gap)

    wide = cols // (4 * LANES) // 2 * 2 * LANES
    small = (cols - 2 * wide) // 2
    if wide and (cols - 2 * wide) % (4 * LANES) == 0:
        if small > wide:
            wide, small = small, wide
        runs = [(0, wide), (2 * wide, small)] if small else [(0, wide)]
    else:
        runs = [(0, cols // 2)]
    units = len(runs)
    u = [Unit(chain, env, h, first, width, order) for h in range(2) for first, width in runs]
    density = None

    def out(run, *parts):
        nonlocal density
        pair = [u[run], u[units + run]]
        amps = [v.other if flip else v.amp for flip in parts for v in pair]
        spec = [(pair[0].order[0], flip) for flip in parts]
        everything = [p for pieces in env["halves"] for p in pieces]
        if runs[run][1] % LANES:
            side = bits[pair[0].order[0]] == 0
            joined = []
            for g in range(2):
                a, b = amps[g], amps[2 + g]
                joined.append(jnp.concatenate([jnp.where(side, a, b), jnp.where(side, b, a)], axis=1))
            amps, spec = joined, [None]
        density = finish(chain, everything, amps, spec, runs[run][0], cols, depth, density)

    def rest_of_factors():
        env["halves"][1] = expand(hold(chain, far_own))

    def gaps(half):
        env["gaps"][half] = stack(chain, env["halves"][1], depth) if half else stack(chain, gap_parts)

    if units == 2:
        for step in PLAN:
            if step[0] == "factors":
                rest_of_factors()
            elif step[0] == "gaps":
                gaps(step[1])
            elif step[0] == "out":
                out(*step[1:])
            else:
                getattr(u[step[1]], step[0])()
    else:
        rest_of_factors()
        gaps(0)
        gaps(1)
        for step in ("start", "keep", "add", "divide", "join"):
            for v in u:
                getattr(v, step)()
        for run in range(units):
            out(run, False, True)
    return density


PLAN = (
    ("start", 0), ("start", 1), ("gaps", 0), ("keep", 0), ("factors",), ("add", 0), ("start", 2), ("keep", 1), ("start", 3),
    ("gaps", 1), ("add", 1), ("divide", 0), ("keep", 2), ("join", 0), ("add", 2), ("divide", 1), ("keep", 3), ("join", 1),
    ("divide", 2), ("add", 3), ("join", 2), ("divide", 3), ("join", 3), ("out", 0, False, True),
    ("out", 1, False), ("out", 1, True),
)


def solution(mesh):
    return jax.shard_map(
        functools.partial(local, mesh.shape["aux"], mesh.shape["orb"]),
        mesh=mesh,
        in_specs=(P("aux", "orb"), P(None, "orb", "aux"), P("orb"), P(None, "orb")),
        out_specs=P("aux", "orb"),
        check_vma=False,
    )
```
